32 devices in a mesh: had: 4 (over z), blk: 8 (over y, x, core).
Axes of the slice: x: 2, y: 2, z: 4, core: 2. Of those that a mesh axis runs over, the one named last changes fastest.
Arguments:
- panel: bfloat16 [65536, 512], P(('had', 'blk')), may hold values from -100 to 100
- signs: int32 [65536], P(('had', 'blk')), may hold values from 0 to 1
- sample_rows: int32 [8, 2048], P('blk'), may hold values from 0 to 8191
Outputs:
- q_panel: bfloat16 [65536, 512], P(('had', 'blk'))
- r_sketch: float32 [512, 512], replicated
- r_gram: float32 [512, 512], replicated
The draws below stay inside these ranges and needn't reach their ends.
All inputs are finite; a program needn't handle non-finite values.
Results may differ from the reference program's by a relative error of at most 0.0075.
The reference program's roundings to bfloat16 on the way (of `sketch_inverse`, `whitened` and `gram_inverse`) count: a program that leaves them out, or rounds other values in their place, can miss the bound.
Values sent between devices are 32-bit elements; how exact they have to be, the bound alone decides.
A program may use at most 448 MiB of HBM per device.

```python
import math
import jax
import jax.numpy as jnp
from jax import lax

K = 512
SK = 2048
LH = 32
R_DEV = 2048
BLOCK_ROWS = 8192
ROWS = 65536
N_HAD = 4
N_BLK = 8


def draw_panel(key, part):
    first_key = jax.random.fold_in(key, 11)
    column_key = jax.random.fold_in(key, 12)
    row_key = jax.random.fold_in(key, 13)
    shared_key = jax.random.fold_in(key, 15)
    pattern_key = jax.random.fold_in(key, 16)
    column_scale = jnp.exp(jax.random.uniform(column_key, (K,), jnp.float32, 0.0, math.log(10.0)))
    row_scale = jnp.exp(jax.random.uniform(row_key, (ROWS,), jnp.float32, 0.0, math.log(3.3)))
    ramp = jnp.exp(math.log(3.0) * jnp.arange(ROWS, dtype=jnp.float32) / ROWS)
    shared = jnp.clip(jax.random.normal(shared_key, (ROWS, 1), jnp.float32), -6.0, 6.0)
    pattern = jax.random.uniform(pattern_key, (1, K), jnp.float32, -1.5, 1.5)
    base = jnp.clip(jax.random.normal(first_key, (ROWS, K), jnp.float32), -6.0, 6.0)
    base = base + 3.5 * shared * pattern
    values = 0.15 * base * column_scale[None, :] * (row_scale * ramp)[:, None]
    values = jnp.clip(values, -100.0, 100.0)
    return values.astype(jnp.bfloat16)


def touch_ends(array, own_key, smallest, top_value):
    extent = array.shape
    place = [jax.random.randint(jax.random.fold_in(own_key, axis), (), 0, extent[axis]) for axis in range(len(extent))]
    array = array.at[tuple(place)].set(smallest)
    longest = extent.index(max(extent))
    place[longest] = (place[longest] + 1) % extent[longest]
    return array.at[tuple(place)].set(top_value)


def setup_inputs(seed: int = 0) -> dict:
    keys = jax.random.split(jax.random.key(seed), 4)
    return {
        "panel": draw_panel(jax.random.fold_in(keys[3], 71), 0),
        "signs": touch_ends(jax.random.randint(keys[1], (ROWS,), 0, 2), jax.random.fold_in(keys[1], 1), 0, 1).astype(jnp.int32),
        "sample_rows": touch_ends(jax.random.randint(keys[2], (N_BLK, SK), 0, BLOCK_ROWS), jax.random.fold_in(keys[2], 1), 0, BLOCK_ROWS - 1).astype(jnp.int32),
    }


def bit_parity(value):
    counted = jnp.zeros_like(value)
    for shift_count in range(16):
        counted = counted + jnp.bitwise_and(jnp.right_shift(value, shift_count), 1)
    return counted % 2

def hadamard(order):
    first = lax.broadcasted_iota(jnp.int32, (order, order), 0)
    second = lax.broadcasted_iota(jnp.int32, (order, order), 1)
    parity = bit_parity(jnp.bitwise_and(first, second))
    return (1 - 2 * parity).astype(jnp.float32)

def upper_factor(matrix):
    return jnp.linalg.cholesky(matrix).T

def lower_inverse(lower):
    order = lower.shape[0]
    inverse = (1.0 / jnp.diagonal(lower)).reshape(order, 1, 1)
    width = 1
    while width < order:
        count = order // (2 * width)
        tiles = lower.reshape(count, 2 * width, count, 2 * width)
        diag_tiles = jnp.moveaxis(jnp.diagonal(tiles, axis1=0, axis2=2), -1, 0)
        corner = diag_tiles[:, width:, :width]
        first_inv = inverse[0::2]
        second_inv = inverse[1::2]
        partial_value = jnp.einsum('ajk,akl->ajl', corner, first_inv, precision=lax.Precision.HIGHEST)
        lower_left = -jnp.einsum('aij,ajl->ail', second_inv, partial_value, precision=lax.Precision.HIGHEST)
        zero_tile = jnp.zeros_like(corner)
        top_half = jnp.concatenate([first_inv, zero_tile], axis=2)
        bottom_half = jnp.concatenate([lower_left, second_inv], axis=2)
        inverse = jnp.concatenate([top_half, bottom_half], axis=1)
        width = width * 2
    return inverse[0]

def inverse_upper(factor):
    return lower_inverse(factor.T).T

def reference(panel, signs, sample_rows):
    groups = R_DEV // LH
    flips = (1 - 2 * signs).astype(jnp.float32)
    blocks = panel.reshape(N_HAD, N_BLK, groups, LH, K)
    flip_blocks = flips.reshape(N_HAD, N_BLK, groups, LH)
    outer = hadamard(N_HAD)
    inner = hadamard(LH)
    factor = 1.0 / math.sqrt(N_HAD * LH * SK * N_BLK)

    def add_block(which, summed):
        member = lax.dynamic_index_in_dim(blocks, which, 1, keepdims=False).astype(jnp.float32)
        member_flips = lax.dynamic_index_in_dim(flip_blocks, which, 1, keepdims=False)
        signed = member * member_flips[..., None]
        mixed = jnp.einsum('ml,hglk->hgmk', inner, signed, precision=lax.Precision.HIGHEST)
        mixed = jnp.einsum('ph,hgmk->pgmk', outer, mixed, precision=lax.Precision.HIGHEST)
        mixed = mixed.reshape(N_HAD * R_DEV, K)
        picks = lax.dynamic_index_in_dim(sample_rows, which, 0, keepdims=False)
        return summed + jnp.take(mixed, picks, axis=0)
    summed = lax.fori_loop(0, N_BLK, add_block, jnp.zeros((SK, K), jnp.float32))
    sketch = summed * factor
    sketch_gram = jnp.dot(sketch.T.astype(jnp.float32), sketch.astype(jnp.float32), precision=lax.Precision.HIGHEST, preferred_element_type=jnp.float32)
    r_sketch = upper_factor(sketch_gram)
    sketch_inverse = inverse_upper(r_sketch).astype(jnp.bfloat16)
    whitened = jnp.dot(panel.astype(jnp.float32), sketch_inverse.astype(jnp.float32), preferred_element_type=jnp.float32).astype(jnp.bfloat16)
    gram = jnp.dot(whitened.T.astype(jnp.float32), whitened.astype(jnp.float32), preferred_element_type=jnp.float32) / ROWS
    r_gram = upper_factor(gram)
    gram_inverse = inverse_upper(r_gram).astype(jnp.bfloat16)
    q_panel = jnp.dot(whitened.astype(jnp.float32), gram_inverse.astype(jnp.float32), preferred_element_type=jnp.float32).astype(jnp.bfloat16)
    return (q_panel, r_sketch, r_gram)
```

```python
import math

import jax
import jax.numpy as jnp
from jax import lax
from jax.experimental import pallas as pl
from jax.experimental.pallas import tpu as pltpu
from jax.sharding import PartitionSpec as P

LH = 32
TILE = 128
STEP = 8
HIGHEST = lax.Precision.HIGHEST


def bit_parity(value):
    counted = jnp.zeros_like(value)
    for shift_count in range(16):
        counted = counted + jnp.bitwise_and(jnp.right_shift(value, shift_count), 1)
    return counted % 2


def factor_tile(tile_ref):
    sub = lax.broadcasted_iota(jnp.int32, (STEP, TILE), 0)
    for start in range(0, TILE, STEP):
        left = tile_ref[start:start + STEP, 0:TILE]
        right = tile_ref[start:start + STEP, TILE:2 * TILE]
        spread = [
            jnp.broadcast_to(left[:, start + j:start + j + 1], (STEP, TILE)) for j in range(STEP)
        ]
        entry = {}
        for j in range(STEP):
            for i in range(j, STEP):
                entry[i, j] = jnp.broadcast_to(spread[j][i:i + 1, :], (STEP, TILE))
        for j in range(STEP):
            pivot = entry[j, j]
            scale = lax.rsqrt(pivot)
            scale = scale * (1.5 - 0.5 * pivot * scale * scale)
            below = {}
            column = jnp.zeros((STEP, TILE), jnp.float32)
            for i in range(j + 1, STEP):
                below[i] = entry[i, j] * scale
                column = jnp.where(sub == i, below[i], column)
            for m in range(j + 1, STEP):
                for i in range(m, STEP):
                    entry[i, m] = entry[i, m] - below[i] * below[m]
            row_left = jnp.broadcast_to(left[j:j + 1, :], (STEP, TILE)) * scale
            row_right = jnp.broadcast_to(right[j:j + 1, :], (STEP, TILE)) * scale
            left = jnp.where(sub == j, row_left, left - column * row_left)
            right = jnp.where(sub == j, row_right, right - column * row_right)
        tile_ref[start:start + STEP, 0:TILE] = left
        tile_ref[start:start + STEP, TILE:2 * TILE] = right
        if start + STEP < TILE:
            both = jnp.concatenate([left, right], axis=1)
            change = lax.dot_general(
                left, both, (((0,), (0,)), ((), ())), precision=HIGHEST,
                preferred_element_type=jnp.float32,
            )
            tile_ref[start + STEP:, :] = tile_ref[start + STEP:, :] - change[start + STEP:, :]


def factor_kernel(scale, matrix_ref, factor_ref, inverse_ref, work, tile):
    order = matrix_ref.shape[0]
    work[:, 0:order] = matrix_ref[...] * scale
    first = lax.broadcasted_iota(jnp.int32, (order, order), 0)
    second = lax.broadcasted_iota(jnp.int32, (order, order), 1)
    work[:, order:] = jnp.where(first == second, 1.0, 0.0)
    tile_first = lax.broadcasted_iota(jnp.int32, (TILE, TILE), 0)
    tile_second = lax.broadcasted_iota(jnp.int32, (TILE, TILE), 1)

    def step(which, carry):
        base = pl.multiple_of(which * TILE, TILE)
        rows = pl.ds(base, TILE)
        tile[:, 0:TILE] = work[rows, rows]
        tile[:, TILE:] = jnp.where(tile_first == tile_second, 1.0, 0.0)
        factor_tile(tile)
        solved = jnp.dot(
            tile[:, TILE:], work[rows, :], precision=HIGHEST, preferred_element_type=jnp.float32
        )
        work[rows, :] = solved
        for other in range(1, order // TILE):
            @pl.when(other > which)
            def _():
                part = slice(other * TILE, (other + 1) * TILE)
                work[part, :] = work[part, :] - lax.dot_general(
                    work[rows, part], work[rows, :], (((0,), (0,)), ((), ())),
                    precision=HIGHEST, preferred_element_type=jnp.float32,
                )
        return carry

    lax.fori_loop(0, order // TILE, step, 0)
    factor_ref[...] = jnp.where(first <= second, work[:, 0:order], 0.0)
    inverse_ref[...] = work[:, order:].astype(jnp.bfloat16)


def factor_and_inverse(matrix, scale, interpret=False):
    order = matrix.shape[0]

    def body(*refs):
        factor_kernel(scale, *refs)

    return pl.pallas_call(
        body,
        out_shape=(
            jax.ShapeDtypeStruct((order, order), jnp.float32),
            jax.ShapeDtypeStruct((order, order), jnp.bfloat16),
        ),
        in_specs=[pl.BlockSpec(memory_space=pltpu.VMEM)],
        out_specs=(pl.BlockSpec(memory_space=pltpu.VMEM),) * 2,
        scratch_shapes=[
            pltpu.VMEM((order, 2 * order), jnp.float32),
            pltpu.VMEM((TILE, 2 * TILE), jnp.float32),
        ],
        interpret=interpret,
    )(matrix)


def sample_kernel(panel_ref, flips_ref, group_ref, index_ref, weight_ref, out_ref, signed, picks):
    rows = panel_ref.shape[0]
    count = group_ref.shape[0]

    @pl.when(pl.program_id(0) == 0)
    def _():
        signed[...] = panel_ref[...] * flips_ref[...].astype(jnp.bfloat16)

    lane = lax.broadcasted_iota(jnp.int32, (count, TILE), 1)
    common = jnp.bitwise_and(jnp.broadcast_to(index_ref[...], (count, TILE)), lane)
    common = jnp.bitwise_xor(common, jnp.right_shift(common, 4))
    common = jnp.bitwise_xor(common, jnp.right_shift(common, 2))
    common = jnp.bitwise_xor(common, jnp.right_shift(common, 1))
    sign = (1 - 2 * jnp.bitwise_and(common, 1)).astype(jnp.float32)
    away = jnp.broadcast_to(group_ref[...], (count, TILE)) - jnp.right_shift(lane, 5)
    per_tile = TILE // LH
    for tile in range(rows // TILE):
        picks[:, tile * TILE:(tile + 1) * TILE] = jnp.where(
            away == tile * per_tile, sign, 0.0
        ).astype(jnp.bfloat16)
    out_ref[...] = weight_ref[...] * jnp.dot(
        picks[...], signed[...], preferred_element_type=jnp.float32
    )


def sample(panel, flips, groups, indices, weights, interpret=False):
    rows, columns = panel.shape
    total = groups.shape[0]
    count = 256
    narrow = pl.BlockSpec((count, 1), lambda i: (i, 0))
    return pl.pallas_call(
        sample_kernel,
        grid=(total // count,),
        out_shape=jax.ShapeDtypeStruct((total, columns), jnp.float32),
        in_specs=[
            pl.BlockSpec((rows, columns), lambda i: (0, 0)),
            pl.BlockSpec((rows, 1), lambda i: (0, 0)),
            narrow, narrow, narrow,
        ],
        out_specs=pl.BlockSpec((count, columns), lambda i: (i, 0)),
        scratch_shapes=[
            pltpu.VMEM((rows, columns), jnp.bfloat16),
            pltpu.VMEM((count, rows), jnp.bfloat16),
        ],
        interpret=interpret,
    )(panel, flips, groups, indices, weights)


def local_sketch(panel, signs, picks, my_group, factor, interpret=False):
    rows_dev = panel.shape[0]
    owners = picks // rows_dev
    offsets = picks % rows_dev
    parity = bit_parity(jnp.bitwise_and(owners, my_group))
    weights = (1 - 2 * parity).astype(jnp.float32) * factor
    flips = (1 - 2 * signs).astype(jnp.float32)
    return sample(
        panel, flips[:, None], (offsets // LH)[:, None], (offsets % LH)[:, None],
        weights[:, None], interpret,
    )


def on_device(panel, signs, sample_rows):
    n_had = lax.axis_size("had")
    n_blk = lax.axis_size("blk")
    my_group = lax.axis_index("had")
    rows_dev, columns = panel.shape
    sketch_count = sample_rows.shape[1]
    factor = 1.0 / math.sqrt(n_had * LH * sketch_count * n_blk)
    partial_sketch = local_sketch(panel, signs, sample_rows[0], my_group, factor)
    sketch = lax.psum(partial_sketch, ("had", "blk"))
    sketch_gram = jnp.dot(
        sketch.T, sketch, precision=HIGHEST, preferred_element_type=jnp.float32
    )
    r_sketch, sketch_inverse = factor_and_inverse(sketch_gram, 1.0)
    across = (((1,), (1,)), ((), ()))
    whitened = lax.dot_general(
        panel, sketch_inverse, across, preferred_element_type=jnp.float32
    ).astype(jnp.bfloat16)
    partial_gram = jnp.einsum("rk,rj->kj", whitened, whitened, preferred_element_type=jnp.float32)
    summed = lax.psum(partial_gram, ("had", "blk"))
    r_gram, gram_inverse = factor_and_inverse(summed, 1.0 / (rows_dev * n_had * n_blk))
    q_panel = lax.dot_general(
        whitened, gram_inverse, across, preferred_element_type=jnp.float32
    ).astype(jnp.bfloat16)
    return (q_panel, r_sketch, r_gram)


def solution(mesh):
    placed = (P(("had", "blk"), None), P(("had", "blk")), P("blk", None))
    return jax.shard_map(
        on_device,
        mesh=mesh,
        in_specs=placed,
        out_specs=(P(("had", "blk"), None), P(), P()),
        check_vma=False,
    )
```

```python
import math

import jax
import jax.numpy as jnp
from jax import lax
from jax.experimental import pallas as pl
from jax.experimental.pallas import tpu as pltpu
from jax.sharding import PartitionSpec as P

LH = 32
TILE = 128
STEP = 8
HIGHEST = lax.Precision.HIGHEST


def bit_parity(value):
    counted = jnp.zeros_like(value)
    for shift_count in range(16):
        counted = counted + jnp.bitwise_and(jnp.right_shift(value, shift_count), 1)
    return counted % 2


def factor_tile(tile_ref):
    sub = lax.broadcasted_iota(jnp.int32, (STEP, TILE), 0)
    for start in range(0, TILE, STEP):
        left = tile_ref[start:start + STEP, 0:TILE]
        right = tile_ref[start:start + STEP, TILE:2 * TILE]
        spread = [
            jnp.broadcast_to(left[:, start + j:start + j + 1], (STEP, TILE)) for j in range(STEP)
        ]
        entry = {}
        for j in range(STEP):
            for i in range(j, STEP):
                entry[i, j] = jnp.broadcast_to(spread[j][i:i + 1, :], (STEP, TILE))
        for j in range(STEP):
            pivot = entry[j, j]
            scale = lax.rsqrt(pivot)
            scale = scale * (1.5 - 0.5 * pivot * scale * scale)
            below = {}
            column = jnp.zeros((STEP, TILE), jnp.float32)
            for i in range(j + 1, STEP):
                below[i] = entry[i, j] * scale
                column = jnp.where(sub == i, below[i], column)
            for m in range(j + 1, STEP):
                for i in range(m, STEP):
                    entry[i, m] = entry[i, m] - below[i] * below[m]
            row_left = jnp.broadcast_to(left[j:j + 1, :], (STEP, TILE)) * scale
            row_right = jnp.broadcast_to(right[j:j + 1, :], (STEP, TILE)) * scale
            left = jnp.where(sub == j, row_left, left - column * row_left)
            right = jnp.where(sub == j, row_right, right - column * row_right)
        tile_ref[start:start + STEP, 0:TILE] = left
        tile_ref[start:start + STEP, TILE:2 * TILE] = right
        if start + STEP < TILE:
            both = jnp.concatenate([left, right], axis=1)
            change = lax.dot_general(
                left, both, (((0,), (0,)), ((), ())), precision=HIGHEST,
                preferred_element_type=jnp.float32,
            )
            tile_ref[start + STEP:, :] = tile_ref[start + STEP:, :] - change[start + STEP:, :]


def factor_kernel(scale, matrix_ref, factor_ref, inverse_ref, work, tile):
    order = matrix_ref.shape[0]
    work[:, 0:order] = matrix_ref[...] * scale
    first = lax.broadcasted_iota(jnp.int32, (order, order), 0)
    second = lax.broadcasted_iota(jnp.int32, (order, order), 1)
    work[:, order:] = jnp.where(first == second, 1.0, 0.0)
    tile_first = lax.broadcasted_iota(jnp.int32, (TILE, TILE), 0)
    tile_second = lax.broadcasted_iota(jnp.int32, (TILE, TILE), 1)

    def step(which, carry):
        base = pl.multiple_of(which * TILE, TILE)
        rows = pl.ds(base, TILE)
        tile[:, 0:TILE] = work[rows, rows]
        tile[:, TILE:] = jnp.where(tile_first == tile_second, 1.0, 0.0)
        factor_tile(tile)
        solved = jnp.dot(
            tile[:, TILE:], work[rows, :], precision=HIGHEST, preferred_element_type=jnp.float32
        )
        work[rows, :] = solved
        for other in range(1, order // TILE):
            @pl.when(other > which)
            def _():
                part = slice(other * TILE, (other + 1) * TILE)
                work[part, :] = work[part, :] - lax.dot_general(
                    work[rows, part], work[rows, :], (((0,), (0,)), ((), ())),
                    precision=HIGHEST, preferred_element_type=jnp.float32,
                )
        return carry

    lax.fori_loop(0, order // TILE, step, 0)
    factor_ref[...] = jnp.where(first <= second, work[:, 0:order], 0.0)
    inverse_ref[...] = work[:, order:].astype(jnp.bfloat16)


def factor_and_inverse(matrix, scale, interpret=False):
    order = matrix.shape[0]

    def body(*refs):
        factor_kernel(scale, *refs)

    return pl.pallas_call(
        body,
        out_shape=(
            jax.ShapeDtypeStruct((order, order), jnp.float32),
            jax.ShapeDtypeStruct((order, order), jnp.bfloat16),
        ),
        in_specs=[pl.BlockSpec(memory_space=pltpu.VMEM)],
        out_specs=(pl.BlockSpec(memory_space=pltpu.VMEM),) * 2,
        scratch_shapes=[
            pltpu.VMEM((order, 2 * order), jnp.float32),
            pltpu.VMEM((TILE, 2 * TILE), jnp.float32),
        ],
        interpret=interpret,
    )(matrix)


def sample_kernel(panel_ref, flips_ref, group_ref, index_ref, weight_ref, out_ref, signed, picks):
    rows = panel_ref.shape[0]
    count = group_ref.shape[0]

    @pl.when(pl.program_id(0) == 0)
    def _():
        signed[...] = panel_ref[...] * flips_ref[...].astype(jnp.bfloat16)

    lane = lax.broadcasted_iota(jnp.int32, (count, TILE), 1)
    common = jnp.bitwise_and(jnp.broadcast_to(index_ref[...], (count, TILE)), lane)
    common = jnp.bitwise_xor(common, jnp.right_shift(common, 4))
    common = jnp.bitwise_xor(common, jnp.right_shift(common, 2))
    common = jnp.bitwise_xor(common, jnp.right_shift(common, 1))
    sign = (1 - 2 * jnp.bitwise_and(common, 1)).astype(jnp.float32)
    away = jnp.broadcast_to(group_ref[...], (count, TILE)) - jnp.right_shift(lane, 5)
    per_tile = TILE // LH
    for tile in range(rows // TILE):
        picks[:, tile * TILE:(tile + 1) * TILE] = jnp.where(
            away == tile * per_tile, sign, 0.0
        ).astype(jnp.bfloat16)
    out_ref[...] = weight_ref[...] * jnp.dot(
        picks[...], signed[...], preferred_element_type=jnp.float32
    )


def sample(panel, flips, groups, indices, weights, interpret=False):
    rows, columns = panel.shape
    total = groups.shape[0]
    count = 256
    narrow = pl.BlockSpec((count, 1), lambda i: (i, 0))
    return pl.pallas_call(
        sample_kernel,
        grid=(total // count,),
        out_shape=jax.ShapeDtypeStruct((total, columns), jnp.float32),
        in_specs=[
            pl.BlockSpec((rows, columns), lambda i: (0, 0)),
            pl.BlockSpec((rows, 1), lambda i: (0, 0)),
            narrow, narrow, narrow,
        ],
        out_specs=pl.BlockSpec((count, columns), lambda i: (i, 0)),
        scratch_shapes=[
            pltpu.VMEM((rows, columns), jnp.bfloat16),
            pltpu.VMEM((count, rows), jnp.bfloat16),
        ],
        interpret=interpret,
    )(panel, flips, groups, indices, weights)


def local_sketch(panel, signs, picks, my_group, factor, interpret=False):
    rows_dev = panel.shape[0]
    owners = picks // rows_dev
    offsets = picks % rows_dev
    parity = bit_parity(jnp.bitwise_and(owners, my_group))
    weights = (1 - 2 * parity).astype(jnp.float32) * factor
    flips = (1 - 2 * signs).astype(jnp.float32)
    return sample(
        panel, flips[:, None], (offsets // LH)[:, None], (offsets % LH)[:, None],
        weights[:, None], interpret,
    )


def mesh_bits(n_had, n_blk):
    bits = []
    for axis, size in (("blk", n_blk), ("had", n_had)):
        mask = 1
        while mask < size:
            bits.append((axis, mask))
            mask *= 2
    return bits


def stream_orders(count):
    plain = list(range(count))
    swapped = list(plain)
    if count > 2:
        swapped[1], swapped[2] = swapped[2], swapped[1]
    return plain, swapped


def halving_count(rows, count):
    halvings = 0
    while halvings < count and (rows >> (halvings + 1)) >= STEP:
        halvings += 1
    return halvings


def recv_bases(rows, count):
    halvings = halving_count(rows, count)
    bases, base = [], 0
    for stage in range(count):
        bases.append(base)
        base += rows >> min(stage + 1, halvings)
    return bases, base


class Exchange:
    def __init__(self, bits, send_sem, recv_sem):
        self.bits = bits
        self.send_sem, self.recv_sem = send_sem, recv_sem
        self.used = 0
        self.mine, self.partner = [], []
        place = {"had": lax.axis_index("had"), "blk": lax.axis_index("blk")}
        for axis, mask in bits:
            bit = (place[axis] // mask) % 2
            other = dict(place)
            other[axis] = place[axis] + mask * (1 - 2 * bit)
            self.mine.append(bit)
            self.partner.append((other["had"], other["blk"]))

    def barrier(self):
        barrier = pltpu.get_barrier_semaphore()
        for partner in self.partner:
            pl.semaphore_signal(
                barrier, inc=1, device_id=partner, device_id_type=pl.DeviceIdType.MESH
            )
        pl.semaphore_wait(barrier, len(self.bits))

    def start(self, which, source, target):
        copy = pltpu.make_async_remote_copy(
            src_ref=source, dst_ref=target,
            send_sem=self.send_sem.at[self.used], recv_sem=self.recv_sem.at[self.used],
            device_id=self.partner[which], device_id_type=pl.DeviceIdType.MESH,
        )
        self.used += 1
        copy.start()
        return copy

    def scatter(self, source, acc, recv, orders, same_rows):
        rows, columns = source.shape
        width = columns // len(orders)
        count = len(self.bits)
        halvings = halving_count(rows, count)
        bases, _ = recv_bases(rows, count)

        def weight(place):
            return rows >> (place + 1)

        def plan(stream, stage):
            order = orders[stream]
            where = (lambda s: order[s]) if same_rows else (lambda s: s)
            fixed = 0
            for s in range(min(stage, halvings)):
                fixed = fixed + self.mine[order[s]] * weight(where(s))
            which = order[stage]
            if stage >= halvings:
                return which, [(fixed, fixed, 0, rows >> halvings)]
            taken = [where(s) for s in range(stage + 1)]
            deepest = max(taken)
            offsets = [0]
            for place in range(deepest):
                if place not in taken:
                    offsets = offsets + [o + weight(place) for o in offsets]
            length = weight(deepest)
            step = weight(where(stage))
            bit = self.mine[which]
            return which, [
                (fixed + o + (1 - bit) * step, fixed + o + bit * step, n * length, length)
                for n, o in enumerate(offsets)
            ]

        def begin(stream, stage):
            which, pieces = plan(stream, stage)
            held = source if stage == 0 else acc
            lanes = slice(stream * width, (stream + 1) * width)
            copies = []
            for send, _, inside, length in pieces:
                copies.append(self.start(
                    which,
                    held.at[pl.ds(pl.multiple_of(send, STEP), length), lanes],
                    recv.at[pl.ds(bases[stage] + inside, length), lanes],
                ))
            return copies

        def finish(stream, stage, copies):
            _, pieces = plan(stream, stage)
            held = source if stage == 0 else acc
            lanes = slice(stream * width, (stream + 1) * width)
            for copy, (_, keep, inside, length) in zip(copies, pieces):
                copy.wait()
                here = pl.ds(pl.multiple_of(keep, STEP), length)
                there = pl.ds(bases[stage] + inside, length)
                acc[here, lanes] = held[here, lanes] + recv[there, lanes]

        streams = range(len(orders))
        flying = [begin(stream, 0) for stream in streams]
        for stage in range(count):
            for stream in streams:
                finish(stream, stage, flying[stream])
                if stage + 1 < count:
                    flying[stream] = begin(stream, stage + 1)
        kept = []
        for order in orders:
            offset = 0
            for s in range(halvings):
                offset = offset + self.mine[order[s]] * weight(order[s] if same_rows else s)
            kept.append(offset)
        return kept

    def gather(self, acc, out, orders, kept):
        rows, columns = out.shape
        width = columns // len(orders)
        halvings = halving_count(rows, len(self.bits))
        kept = list(kept)
        flying = [None] * len(orders)
        streams = range(len(orders))

        def begin(stream, stage):
            lanes = slice(stream * width, (stream + 1) * width)
            region = pl.ds(pl.multiple_of(kept[stream], STEP), rows >> (stage + 1))
            flying[stream] = self.start(
                orders[stream][stage], out.at[region, lanes], out.at[region, lanes]
            )

        for stream in streams:
            lanes = slice(stream * width, (stream + 1) * width)
            region = pl.ds(pl.multiple_of(kept[stream], STEP), rows >> halvings)
            out[region, lanes] = acc[region, lanes]
            begin(stream, halvings - 1)
        for stage in reversed(range(halvings)):
            for stream in streams:
                flying[stream].wait()
                kept[stream] = kept[stream] - self.mine[orders[stream][stage]] * (rows >> (stage + 1))
                if stage:
                    begin(stream, stage - 1)


def sketch_gram_sum(partial, n_had, n_blk):
    rows, columns = partial.shape
    bits = mesh_bits(n_had, n_blk)
    count = len(bits)
    orders = stream_orders(count)
    own = rows >> count
    copies = 8 * count + 8

    def body(in_ref, out_ref, acc, recv, part, total, landed, send_sem, recv_sem):
        exchange = Exchange(bits, send_sem, recv_sem)
        exchange.barrier()
        kept = exchange.scatter(in_ref, acc, recv, orders, True)
        mine = acc[pl.ds(pl.multiple_of(kept[0], STEP), own), :]
        part[...] = lax.dot_general(
            mine, mine, (((0,), (0,)), ((), ())), precision=HIGHEST,
            preferred_element_type=jnp.float32,
        )
        kept = exchange.scatter(part, total, landed, orders, False)
        exchange.gather(total, out_ref, orders, kept)

    return pl.pallas_call(
        body,
        out_shape=jax.ShapeDtypeStruct((columns, columns), jnp.float32),
        in_specs=[pl.BlockSpec(memory_space=pltpu.VMEM)],
        out_specs=pl.BlockSpec(memory_space=pltpu.VMEM),
        scratch_shapes=[
            pltpu.VMEM((rows, columns), jnp.float32),
            pltpu.VMEM((recv_bases(rows, count)[1], columns), jnp.float32),
            pltpu.VMEM((columns, columns), jnp.float32),
            pltpu.VMEM((columns, columns), jnp.float32),
            pltpu.VMEM((recv_bases(columns, count)[1], columns), jnp.float32),
            pltpu.SemaphoreType.DMA((copies,)),
            pltpu.SemaphoreType.DMA((copies,)),
        ],
        compiler_params=pltpu.CompilerParams(collective_id=0, has_side_effects=True),
    )(partial)


def matrix_sum(partial, n_had, n_blk):
    rows, columns = partial.shape
    bits = mesh_bits(n_had, n_blk)
    count = len(bits)
    orders = stream_orders(count)
    copies = 4 * count + 4

    def body(in_ref, out_ref, total, landed, send_sem, recv_sem):
        exchange = Exchange(bits, send_sem, recv_sem)
        exchange.barrier()
        kept = exchange.scatter(in_ref, total, landed, orders, False)
        exchange.gather(total, out_ref, orders, kept)

    return pl.pallas_call(
        body,
        out_shape=jax.ShapeDtypeStruct((rows, columns), jnp.float32),
        in_specs=[pl.BlockSpec(memory_space=pltpu.VMEM)],
        out_specs=pl.BlockSpec(memory_space=pltpu.VMEM),
        scratch_shapes=[
            pltpu.VMEM((rows, columns), jnp.float32),
            pltpu.VMEM((recv_bases(rows, count)[1], columns), jnp.float32),
            pltpu.SemaphoreType.DMA((copies,)),
            pltpu.SemaphoreType.DMA((copies,)),
        ],
        compiler_params=pltpu.CompilerParams(collective_id=1, has_side_effects=True),
    )(partial)


def on_device(panel, signs, sample_rows):
    n_had = lax.axis_size("had")
    n_blk = lax.axis_size("blk")
    my_group = lax.axis_index("had")
    rows_dev, columns = panel.shape
    sketch_count = sample_rows.shape[1]
    factor = 1.0 / math.sqrt(n_had * LH * sketch_count * n_blk)
    partial_sketch = local_sketch(panel, signs, sample_rows[0], my_group, factor)
    sketch_gram = sketch_gram_sum(partial_sketch, n_had, n_blk)
    r_sketch, sketch_inverse = factor_and_inverse(sketch_gram, 1.0)
    across = (((1,), (1,)), ((), ()))
    whitened = lax.dot_general(
        panel, sketch_inverse, across, preferred_element_type=jnp.float32
    ).astype(jnp.bfloat16)
    partial_gram = jnp.einsum("rk,rj->kj", whitened, whitened, preferred_element_type=jnp.float32)
    summed = matrix_sum(partial_gram, n_had, n_blk)
    r_gram, gram_inverse = factor_and_inverse(summed, 1.0 / (rows_dev * n_had * n_blk))
    q_panel = lax.dot_general(
        whitened, gram_inverse, across, preferred_element_type=jnp.float32
    ).astype(jnp.bfloat16)
    return (q_panel, r_sketch, r_gram)


def solution(mesh):
    placed = (P(("had", "blk"), None), P(("had", "blk")), P("blk", None))
    return jax.shard_map(
        on_device,
        mesh=mesh,
        in_specs=placed,
        out_specs=(P(("had", "blk"), None), P(), P()),
        check_vma=False,
    )
```

```python
import math

import jax
import jax.numpy as jnp
from jax import lax
from jax.experimental import pallas as pl
from jax.experimental.pallas import tpu as pltpu
from jax.sharding import PartitionSpec as P

LH = 32
TILE = 128
STEP = 8
SUPER = 32
HIGHEST = lax.Precision.HIGHEST


def factor_tile(tile_ref):
    sub = lax.broadcasted_iota(jnp.int32, (STEP, TILE), 0)
    shape = (STEP, TILE)
    for base in range(0, TILE, SUPER):
        parts = SUPER // STEP
        left = [tile_ref[base + p * STEP:base + (p + 1) * STEP, 0:TILE] for p in range(parts)]
        right = [tile_ref[base + p * STEP:base + (p + 1) * STEP, TILE:] for p in range(parts)]
        for now in range(parts):
            start = base + now * STEP
            rest = range(now + 1, parts)
            spread = {
                (p, j): jnp.broadcast_to(left[p][:, start + j:start + j + 1], shape)
                for j in range(STEP) for p in range(now, parts)
            }
            entry = {
                (i, j): jnp.broadcast_to(spread[now, j][i:i + 1, :], shape)
                for j in range(STEP) for i in range(j, STEP)
            }
            for j in range(STEP):
                pivot = entry[j, j]
                scale = lax.rsqrt(pivot)
                scale = scale * (1.5 - 0.5 * pivot * scale * scale)
                below = {}
                column = jnp.zeros(shape, jnp.float32)
                for i in range(j + 1, STEP):
                    below[i] = entry[i, j] * scale
                    column = jnp.where(sub == i, below[i], column)
                for m in range(j + 1, STEP):
                    for i in range(m, STEP):
                        entry[i, m] = entry[i, m] - below[i] * below[m]
                row_left = jnp.broadcast_to(left[now][j:j + 1, :], shape) * scale
                row_right = jnp.broadcast_to(right[now][j:j + 1, :], shape) * scale
                left[now] = jnp.where(sub == j, row_left, left[now] - column * row_left)
                right[now] = jnp.where(sub == j, row_right, right[now] - column * row_right)
                for p in rest:
                    outer = spread[p, j] * scale
                    for m in range(j + 1, STEP):
                        spread[p, m] = spread[p, m] - outer * below[m]
                    left[p] = left[p] - outer * row_left
                    right[p] = right[p] - outer * row_right
        lefts = jnp.concatenate(left, axis=0)
        rights = jnp.concatenate(right, axis=0)
        tile_ref[base:base + SUPER, 0:TILE] = lefts
        tile_ref[base:base + SUPER, TILE:] = rights
        if base + SUPER < TILE:
            both = jnp.concatenate([lefts, rights], axis=1)
            change = lax.dot_general(
                lefts, both, (((0,), (0,)), ((), ())), precision=HIGHEST,
                preferred_element_type=jnp.float32,
            )
            tile_ref[base + SUPER:, :] = tile_ref[base + SUPER:, :] - change[base + SUPER:, :]


def factor_kernel(scale, matrix_ref, factor_ref, inverse_ref, work, tile):
    order = matrix_ref.shape[0]
    work[:, 0:order] = matrix_ref[...] * scale
    first = lax.broadcasted_iota(jnp.int32, (order, order), 0)
    second = lax.broadcasted_iota(jnp.int32, (order, order), 1)
    work[:, order:] = jnp.where(first == second, 1.0, 0.0)
    tile_first = lax.broadcasted_iota(jnp.int32, (TILE, TILE), 0)
    tile_second = lax.broadcasted_iota(jnp.int32, (TILE, TILE), 1)

    def step(which, carry):
        base = pl.multiple_of(which * TILE, TILE)
        rows = pl.ds(base, TILE)
        tile[:, 0:TILE] = work[rows, rows]
        tile[:, TILE:] = jnp.where(tile_first == tile_second, 1.0, 0.0)
        factor_tile(tile)
        solved = jnp.dot(
            tile[:, TILE:], work[rows, :], precision=HIGHEST, preferred_element_type=jnp.float32
        )
        work[rows, :] = solved
        for other in range(1, order // TILE):
            @pl.when(other > which)
            def _():
                part = slice(other * TILE, (other + 1) * TILE)
                work[part, :] = work[part, :] - lax.dot_general(
                    work[rows, part], work[rows, :], (((0,), (0,)), ((), ())),
                    precision=HIGHEST, preferred_element_type=jnp.float32,
                )
        return carry

    lax.fori_loop(0, order // TILE, step, 0)
    factor_ref[...] = jnp.where(first <= second, work[:, 0:order], 0.0)
    inverse_ref[...] = work[:, order:].astype(jnp.bfloat16)


def factor_and_inverse(matrix, scale, interpret=False):
    order = matrix.shape[0]

    def body(*refs):
        factor_kernel(scale, *refs)

    return pl.pallas_call(
        body,
        out_shape=(
            jax.ShapeDtypeStruct((order, order), jnp.float32),
            jax.ShapeDtypeStruct((order, order), jnp.bfloat16),
        ),
        in_specs=[pl.BlockSpec(memory_space=pltpu.VMEM)],
        out_specs=(pl.BlockSpec(memory_space=pltpu.VMEM),) * 2,
        scratch_shapes=[
            pltpu.VMEM((order, 2 * order), jnp.float32),
            pltpu.VMEM((TILE, 2 * TILE), jnp.float32),
        ],
        interpret=interpret,
    )(matrix)


def sample_kernel(factor, panel_ref, signs_ref, picks_ref, out_ref, signed, chosen):
    rows = panel_ref.shape[0]
    count = picks_ref.shape[0]

    @pl.when(pl.program_id(0) == 0)
    def _():
        flips = (1 - 2 * signs_ref[...]).astype(jnp.float32).astype(jnp.bfloat16)
        signed[...] = panel_ref[...] * flips

    def sign_of(value, shifts):
        for shift in shifts:
            value = jnp.bitwise_xor(value, jnp.right_shift(value, shift))
        return (1 - 2 * jnp.bitwise_and(value, 1)).astype(jnp.float32)

    picks = jnp.broadcast_to(picks_ref[...], (count, TILE))
    lane = lax.broadcasted_iota(jnp.int32, (count, TILE), 1)
    owners = picks // rows
    offsets = picks - owners * rows
    groups = offsets // LH
    indices = offsets - groups * LH
    sign = sign_of(jnp.bitwise_and(indices, lane), (4, 2, 1))
    outer = sign_of(jnp.bitwise_and(owners, lax.axis_index("had")), (8, 4, 2, 1))
    weights = outer[:, 0:1] * factor
    away = groups - lane // LH
    for tile in range(rows // TILE):
        chosen[:, tile * TILE:(tile + 1) * TILE] = jnp.where(
            away == tile * (TILE // LH), sign, 0.0
        ).astype(jnp.bfloat16)
    out_ref[...] = weights * jnp.dot(
        chosen[...], signed[...], preferred_element_type=jnp.float32
    )


def local_sketch(panel, signs, picks, factor):
    rows, columns = panel.shape
    total = picks.shape[0]
    count = 256

    def body(*refs):
        sample_kernel(factor, *refs)

    return pl.pallas_call(
        body,
        grid=(total // count,),
        out_shape=jax.ShapeDtypeStruct((total, columns), jnp.float32),
        in_specs=[
            pl.BlockSpec((rows, columns), lambda i: (0, 0)),
            pl.BlockSpec((rows, 1), lambda i: (0, 0)),
            pl.BlockSpec((count, 1), lambda i: (i, 0)),
        ],
        out_specs=pl.BlockSpec((count, columns), lambda i: (i, 0)),
        scratch_shapes=[
            pltpu.VMEM((rows, columns), jnp.bfloat16),
            pltpu.VMEM((count, rows), jnp.bfloat16),
        ],
    )(panel, signs[:, None], picks[:, None])


def mesh_bits(n_had, n_blk):
    bits = []
    for axis, size in (("blk", n_blk), ("had", n_had)):
        mask = 1
        while mask < size:
            bits.append((axis, mask))
            mask *= 2
    return bits


def stream_orders(count):
    plain = list(range(count))
    swapped = list(plain)
    if count > 2:
        swapped[1], swapped[2] = swapped[2], swapped[1]
    return plain, swapped


def halving_count(rows, count):
    halvings = 0
    while halvings < count and (rows >> (halvings + 1)) >= STEP:
        halvings += 1
    return halvings


def recv_bases(rows, count):
    halvings = halving_count(rows, count)
    bases, base = [], 0
    for stage in range(count):
        bases.append(base)
        base += rows >> min(stage + 1, halvings)
    return bases, base


class Exchange:
    def __init__(self, bits, send_sem, recv_sem):
        self.bits = bits
        self.send_sem, self.recv_sem = send_sem, recv_sem
        self.used = 0
        self.mine, self.partner = [], []
        place = {"had": lax.axis_index("had"), "blk": lax.axis_index("blk")}
        for axis, mask in bits:
            bit = (place[axis] // mask) % 2
            other = dict(place)
            other[axis] = place[axis] + mask * (1 - 2 * bit)
            self.mine.append(bit)
            self.partner.append((other["had"], other["blk"]))

    def barrier(self):
        barrier = pltpu.get_barrier_semaphore()
        for partner in self.partner:
            pl.semaphore_signal(
                barrier, inc=1, device_id=partner, device_id_type=pl.DeviceIdType.MESH
            )
        pl.semaphore_wait(barrier, len(self.bits))

    def start(self, which, source, target):
        copy = pltpu.make_async_remote_copy(
            src_ref=source, dst_ref=target,
            send_sem=self.send_sem.at[self.used], recv_sem=self.recv_sem.at[self.used],
            device_id=self.partner[which], device_id_type=pl.DeviceIdType.MESH,
        )
        self.used += 1
        copy.start()
        return copy

    def scatter(self, source, acc, recv, orders, same_rows):
        rows, columns = source.shape
        width = columns // len(orders)
        count = len(self.bits)
        halvings = halving_count(rows, count)
        bases, _ = recv_bases(rows, count)

        def weight(place):
            return rows >> (place + 1)

        def plan(stream, stage):
            order = orders[stream]
            where = (lambda s: order[s]) if same_rows else (lambda s: s)
            fixed = 0
            for s in range(min(stage, halvings)):
                fixed = fixed + self.mine[order[s]] * weight(where(s))
            which = order[stage]
            if stage >= halvings:
                return which, [(fixed, fixed, 0, rows >> halvings)]
            taken = [where(s) for s in range(stage + 1)]
            deepest = max(taken)
            offsets = [0]
            for place in range(deepest):
                if place not in taken:
                    offsets = offsets + [o + weight(place) for o in offsets]
            length = weight(deepest)
            step = weight(where(stage))
            bit = self.mine[which]
            return which, [
                (fixed + o + (1 - bit) * step, fixed + o + bit * step, n * length, length)
                for n, o in enumerate(offsets)
            ]

        def begin(stream, stage):
            which, pieces = plan(stream, stage)
            held = source if stage == 0 else acc
            lanes = slice(stream * width, (stream + 1) * width)
            copies = []
            for send, _, inside, length in pieces:
                copies.append(self.start(
                    which,
                    held.at[pl.ds(pl.multiple_of(send, STEP), length), lanes],
                    recv.at[pl.ds(bases[stage] + inside, length), lanes],
                ))
            return copies

        def finish(stream, stage, copies):
            _, pieces = plan(stream, stage)
            held = source if stage == 0 else acc
            lanes = slice(stream * width, (stream + 1) * width)
            for copy, (_, keep, inside, length) in zip(copies, pieces):
                copy.wait()
                here = pl.ds(pl.multiple_of(keep, STEP), length)
                there = pl.ds(bases[stage] + inside, length)
                acc[here, lanes] = held[here, lanes] + recv[there, lanes]

        streams = range(len(orders))
        flying = [begin(stream, 0) for stream in streams]
        for stage in range(count):
            for stream in streams:
                finish(stream, stage, flying[stream])
                if stage + 1 < count:
                    flying[stream] = begin(stream, stage + 1)
        kept = []
        for order in orders:
            offset = 0
            for s in range(halvings):
                offset = offset + self.mine[order[s]] * weight(order[s] if same_rows else s)
            kept.append(offset)
        return kept

    def gather(self, acc, out, orders, kept):
        rows, columns = out.shape
        width = columns // len(orders)
        halvings = halving_count(rows, len(self.bits))
        kept = list(kept)
        flying = [None] * len(orders)
        streams = range(len(orders))

        def begin(stream, stage):
            lanes = slice(stream * width, (stream + 1) * width)
            region = pl.ds(pl.multiple_of(kept[stream], STEP), rows >> (stage + 1))
            flying[stream] = self.start(
                orders[stream][stage], out.at[region, lanes], out.at[region, lanes]
            )

        for stream in streams:
            lanes = slice(stream * width, (stream + 1) * width)
            region = pl.ds(pl.multiple_of(kept[stream], STEP), rows >> halvings)
            out[region, lanes] = acc[region, lanes]
            begin(stream, halvings - 1)
        for stage in reversed(range(halvings)):
            for stream in streams:
                flying[stream].wait()
                kept[stream] = kept[stream] - self.mine[orders[stream][stage]] * (rows >> (stage + 1))
                if stage:
                    begin(stream, stage - 1)


def sketch_gram_sum(partial, n_had, n_blk):
    rows, columns = partial.shape
    bits = mesh_bits(n_had, n_blk)
    count = len(bits)
    orders = stream_orders(count)
    own = rows >> count
    copies = 8 * count + 8

    def body(in_ref, out_ref, acc, recv, part, total, landed, send_sem, recv_sem):
        exchange = Exchange(bits, send_sem, recv_sem)
        exchange.barrier()
        kept = exchange.scatter(in_ref, acc, recv, orders, True)
        mine = acc[pl.ds(pl.multiple_of(kept[0], STEP), own), :]
        part[...] = lax.dot_general(
            mine, mine, (((0,), (0,)), ((), ())), precision=HIGHEST,
            preferred_element_type=jnp.float32,
        )
        kept = exchange.scatter(part, total, landed, orders, False)
        exchange.gather(total, out_ref, orders, kept)

    return pl.pallas_call(
        body,
        out_shape=jax.ShapeDtypeStruct((columns, columns), jnp.float32),
        in_specs=[pl.BlockSpec(memory_space=pltpu.VMEM)],
        out_specs=pl.BlockSpec(memory_space=pltpu.VMEM),
        scratch_shapes=[
            pltpu.VMEM((rows, columns), jnp.float32),
            pltpu.VMEM((recv_bases(rows, count)[1], columns), jnp.float32),
            pltpu.VMEM((columns, columns), jnp.float32),
            pltpu.VMEM((columns, columns), jnp.float32),
            pltpu.VMEM((recv_bases(columns, count)[1], columns), jnp.float32),
            pltpu.SemaphoreType.DMA((copies,)),
            pltpu.SemaphoreType.DMA((copies,)),
        ],
        compiler_params=pltpu.CompilerParams(collective_id=0, has_side_effects=True),
    )(partial)


def matrix_sum(partial, n_had, n_blk):
    rows, columns = partial.shape
    bits = mesh_bits(n_had, n_blk)
    count = len(bits)
    orders = stream_orders(count)
    copies = 4 * count + 4

    def body(in_ref, out_ref, total, landed, send_sem, recv_sem):
        exchange = Exchange(bits, send_sem, recv_sem)
        exchange.barrier()
        kept = exchange.scatter(in_ref, total, landed, orders, False)
        exchange.gather(total, out_ref, orders, kept)

    return pl.pallas_call(
        body,
        out_shape=jax.ShapeDtypeStruct((rows, columns), jnp.float32),
        in_specs=[pl.BlockSpec(memory_space=pltpu.VMEM)],
        out_specs=pl.BlockSpec(memory_space=pltpu.VMEM),
        scratch_shapes=[
            pltpu.VMEM((rows, columns), jnp.float32),
            pltpu.VMEM((recv_bases(rows, count)[1], columns), jnp.float32),
            pltpu.SemaphoreType.DMA((copies,)),
            pltpu.SemaphoreType.DMA((copies,)),
        ],
        compiler_params=pltpu.CompilerParams(collective_id=1, has_side_effects=True),
    )(partial)


def on_device(panel, signs, sample_rows):
    n_had = lax.axis_size("had")
    n_blk = lax.axis_size("blk")
    rows_dev, columns = panel.shape
    sketch_count = sample_rows.shape[1]
    factor = 1.0 / math.sqrt(n_had * LH * sketch_count * n_blk)
    partial_sketch = local_sketch(panel, signs, sample_rows[0], factor)
    sketch_gram = sketch_gram_sum(partial_sketch, n_had, n_blk)
    r_sketch, sketch_inverse = factor_and_inverse(sketch_gram, 1.0)
    across = (((1,), (1,)), ((), ()))
    whitened = lax.dot_general(
        panel, sketch_inverse, across, preferred_element_type=jnp.float32
    ).astype(jnp.bfloat16)
    partial_gram = jnp.einsum("rk,rj->kj", whitened, whitened, preferred_element_type=jnp.float32)
    summed = matrix_sum(partial_gram, n_had, n_blk)
    r_gram, gram_inverse = factor_and_inverse(summed, 1.0 / (rows_dev * n_had * n_blk))
    q_panel = lax.dot_general(
        whitened, gram_inverse, across, preferred_element_type=jnp.float32
    ).astype(jnp.bfloat16)
    return (q_panel, r_sketch, r_gram)


def solution(mesh):
    placed = (P(("had", "blk"), None), P(("had", "blk")), P("blk", None))
    return jax.shard_map(
        on_device,
        mesh=mesh,
        in_specs=placed,
        out_specs=(P(("had", "blk"), None), P(), P()),
        check_vma=False,
    )
```
